768 devices in a mesh: section: 16 (over x, y_hi, core), tp: 48 (over y_lo, z).
Axes of the slice: x: 4, y: 8 (y_hi: 2, y_lo: 4; y = y_hi * 4 + y_lo), z: 12, core: 2. Of those that a mesh axis runs over, the one named last changes fastest.
Arguments:
- grad_attn: bfloat16 [16, 48, 128, 128], P('section', 'tp'), may hold values from -6 to 6
- w_value: bfloat16 [16, 12288, 6144], P('section', 'tp'), may hold values from -0.0546875 to 0.0546875
- probs_own: bfloat16 [16, 48, 128, 128], P('section', 'tp'), may hold values from 0.0009994507 to 0.25
- probs_spare: bfloat16 [16, 48, 128, 128], P('section', 'tp'), may hold values from 0.0009994507 to 0.25
- evicted: int32 [16, 4], P('section'), may hold values from 0 to 1, as said below
- layer_input: bfloat16 [16, 128, 12288], P('section', None, 'tp'), may hold values from -6 to 6
- gain: float32 [16, 12288], P('section', 'tp'), may hold values from 0.1 to 1.9
Outputs:
- handed: bfloat16 [16, 128, 12288], P('section', None, 'tp')
The draws below stay inside these ranges and needn't reach their ends.
Inputs may be any that keep to these rules, and one draw needn't show every extreme that they name: Section 0 has every tile evicted.
All inputs are finite; a program needn't handle non-finite values.
Results may differ from the reference program's by a relative error of at most 0.0049.
Values may be sent and summed in bfloat16 or wider, within the bound.
A program may use at most 32 MiB of HBM per device.

```python
import math
import jax
import jax.numpy as jnp
from jax import lax

D = 12288
HD = 128
TOK = 128
TILES = 4
SECTIONS = 16
HEADS = 48


def draw_evicted(key, part):
    values = jax.random.randint(key, (SECTIONS, TILES), 0, SECTIONS)
    section_rows = lax.broadcasted_iota(jnp.int32, (SECTIONS, TILES), 0)
    return (values >= section_rows).astype(jnp.int32)


def shard_levels(stream_key, extent, pieces, smallest, top_value):
    loudness, own = 1.0, jax.random.fold_in(stream_key, 6)
    for axis_at, shards_of in pieces:
        heights = jnp.exp(jax.random.uniform(jax.random.fold_in(own, axis_at), (shards_of,), jnp.float32, smallest / len(pieces), top_value / len(pieces)))
        loudness = loudness * jnp.repeat(heights, extent[axis_at] // shards_of).reshape([-1 if axis == axis_at else 1 for axis in range(len(extent))])
    return loudness


def noise(rng, shape, scale, limit, pieces=(), held_as=jnp.bfloat16):
    entries = scale * jax.random.normal(rng, shape, jnp.float32)
    if pieces:
        entries = entries * shard_levels(rng, shape, pieces, -0.22, 0.18)
    return jnp.clip(entries, -limit, limit).astype(held_as)


def setup_inputs(seed: int = 0) -> dict:
    splits = jax.random.split(jax.random.key(seed), 8)
    return {
        "grad_attn": noise(splits[0], (SECTIONS, HEADS, TOK, HD), 1.0, 6.0, ((0, 16), (1, 48))),
        "w_value": noise(splits[1], (SECTIONS, D, HEADS * HD), D ** -0.5, 0.0546875, ((0, 16), (1, 48))),
        "probs_own": jnp.clip(jnp.exp(math.log(0.25) - 5.5220104 * jax.random.uniform(splits[2], (SECTIONS, HEADS, TOK, TOK), jnp.float32) ** shard_levels(splits[2], (SECTIONS, HEADS, TOK, TOK), ((0, 16), (1, 48)), -0.2, 0.2)), 0.0009994507, 0.25).astype(jnp.bfloat16),
        "probs_spare": jnp.clip(jnp.exp(math.log(0.25) - 5.5220104 * jax.random.uniform(splits[3], (SECTIONS, HEADS, TOK, TOK), jnp.float32) ** shard_levels(splits[3], (SECTIONS, HEADS, TOK, TOK), ((0, 16), (1, 48)), -0.2, 0.2)), 0.0009994507, 0.25).astype(jnp.bfloat16),
        "evicted": draw_evicted(jax.random.fold_in(splits[7], 71), 0),
        "layer_input": noise(splits[5], (SECTIONS, TOK, D), 1.0, 6.0, ((0, 16), (2, 48))),
        "gain": jnp.clip(1.0 + 0.18 * jax.random.normal(splits[6], (SECTIONS, D), jnp.float32), 0.1, 1.9),
    }


def section_branch(args):
    grad_attn, weights, probs, flags, spare, inputs, gain = args
    mixed = jnp.where(flags[None, :, None] == 1, spare, probs)
    grad_value = jnp.einsum('hqk,hqd->hkd', mixed.astype(jnp.float32), grad_attn.astype(jnp.float32)).astype(jnp.bfloat16)
    flat = jnp.transpose(grad_value, (1, 0, 2)).reshape(TOK, HEADS * HD)
    grad_normed = jnp.dot(flat, weights.T, preferred_element_type=jnp.float32)
    values = inputs.astype(jnp.float32)
    squares = lax.optimization_barrier(jnp.sum(values * values, axis=1))
    inv = 1.0 / jnp.sqrt(squares / D + 1e-05)
    inner = lax.optimization_barrier(jnp.sum(gain[None, :] * grad_normed * values, axis=1))
    branch = gain[None, :] * grad_normed * inv[:, None] - values * (inner * inv ** 3 / D)[:, None]
    return branch.astype(jnp.bfloat16)

def reference(grad_attn, w_value, probs_own, probs_spare, evicted, layer_input, gain):
    flags = jnp.repeat(evicted, TOK // TILES, axis=1)
    spare = jnp.roll(probs_spare, -(SECTIONS // 2), axis=0)
    branch = lax.map(section_branch, (grad_attn, w_value, probs_own, flags, spare, layer_input, gain))
    return jnp.roll(branch, -1, axis=0)
```

```python
import functools

import jax
import jax.numpy as jnp
from jax import lax
from jax.experimental import pallas as pl
from jax.experimental.pallas import tpu as pltpu
from jax.sharding import PartitionSpec as P

RUN = 4
MESH = pl.DeviceIdType.MESH


def kernel(
    sizes,
    ga_h,
    w_h,
    own_h,
    spare_h,
    ev_h,
    x_h,
    gain_h,
    out_ref,
    ga_v,
    w_v,
    own_v,
    spare_v,
    ev_s,
    x_v,
    gain_v,
    xr_v,
    gath,
    acc,
    a_send,
    a_recv,
    red_loc,
    red_y,
    red_col,
    red_z,
    lsem,
    hsem,
    y_ss,
    ring_ss,
    rsem,
    ry_ss,
    ry_rs,
    rz_ss,
    rz_rs,
):
    sections, ny, nz, width = sizes
    tok = own_h.shape[2]
    tiles = ev_h.shape[1]
    rows = tok // tiles
    feats = w_h.shape[1]
    hd = ga_h.shape[3]
    s = lax.axis_index("section")
    t = lax.axis_index("tp")
    y, z = t // nz, t % nz
    before = (s + sections - 1) % sections
    after = (s + 1) % sections
    across = (s + sections // 2) % sections
    right = y * nz + (z + 1) % nz
    left = y * nz + (z + nz - 1) % nz

    def dev(section, tp):
        return {"section": section, "tp": tp}

    barrier = pltpu.get_barrier_semaphore()
    sources = [dev(across, t), dev(s, right), dev(s, left)]
    sources += [dev(s, ((y + i) % ny) * nz + z) for i in range(1, ny)]
    sources += [dev(after, y * nz + (z + i) % nz) for i in range(nz)]
    for d in sources:
        pl.semaphore_signal(barrier, inc=1, device_id=d, device_id_type=MESH)

    local = [
        pltpu.make_async_copy(own_h.at[0, 0], own_v, lsem.at[0]),
        pltpu.make_async_copy(ga_h.at[0, 0], ga_v, lsem.at[1]),
        pltpu.make_async_copy(ev_h, ev_s, lsem.at[2]),
        pltpu.make_async_copy(x_h.at[0], x_v, lsem.at[3]),
        pltpu.make_async_copy(gain_h, gain_v, lsem.at[4]),
        pltpu.make_async_copy(w_h.at[0], w_v, lsem.at[5]),
    ]
    for c in local:
        c.start()
    pl.semaphore_wait(barrier, len(sources))

    def remote(src, dst, send, recv, d):
        return pltpu.make_async_remote_copy(
            src_ref=src, dst_ref=dst, send_sem=send, recv_sem=recv, device_id=d, device_id_type=MESH
        )

    spare_c = remote(spare_h.at[0, 0], spare_v, hsem.at[0], hsem.at[1], dev(across, t))
    spare_c.start()
    x_c = remote(x_h.at[0], xr_v, hsem.at[2], hsem.at[3], dev(before, t))
    x_c.start()

    for c in local[:5]:
        c.wait()

    def token_row(v):
        half = v[:, :128]
        for i in range(128, feats, 128):
            half = half + v[:, i : i + 128]
        return jnp.sum(half.T, axis=0, keepdims=True)

    xf = x_v[...].astype(jnp.float32)
    red_loc[...] = jnp.zeros(red_loc.shape, jnp.float32)
    red_loc[0:1, :] = token_row(xf * xf)

    spare_c.wait_recv()
    parts = []
    for i in range(tiles):
        flag = jnp.full((rows, tok), ev_s[0, i], jnp.int32)
        parts.append(
            jnp.where(
                flag == 1,
                spare_v[i * rows : (i + 1) * rows, :].astype(jnp.float32),
                own_v[i * rows : (i + 1) * rows, :].astype(jnp.float32),
            )
        )
    mixed = jnp.concatenate(parts, axis=0)
    turned = mixed.T.astype(jnp.bfloat16)
    gath[t] = jnp.dot(turned, ga_v[...], preferred_element_type=jnp.float32).astype(jnp.bfloat16)

    def along(j, way):
        return remote(gath.at[j], gath.at[j], ring_ss.at[way, j], rsem.at[j], dev(s, (right, left)[way]))

    def arrived(j):
        along(j, 0).wait_recv()

    def peer(i):
        return ((y + i) % ny) * nz + z

    def share(i):
        return remote(gath.at[t], gath.at[t], y_ss.at[i], rsem.at[t], dev(s, peer(i)))

    along(t, 0).start()
    along(t, 1).start()
    for i in range(1, ny):
        share(i).start()
    local[5].wait()
    for i in range(1, ny):
        arrived(peer(i))
        along(peer(i), 0).start()
        along(peer(i), 1).start()

    def product(heads):
        lhs = jnp.concatenate([gath[j] for j in heads], axis=1)
        rhs = jnp.concatenate([w_v[:, pl.ds(pl.multiple_of(j * hd, hd), hd)] for j in heads], axis=1)
        return lax.dot_general(lhs, rhs, (((1,), (1,)), ((), ())), preferred_element_type=jnp.float32)

    acc[...] = product([peer(i) for i in range(ny)])

    half = nz // 2

    def step(k, last):
        from_left = (z + nz - k) % nz
        from_right = (z + k) % nz
        heads = []
        for i in range(ny):
            base = ((y + i) % ny) * nz
            arrived(base + from_left)
            if not last or i % 2 == 0:
                along(base + from_left, 0).start()
            arrived(base + from_right)
            if not last or i % 2 == 1:
                along(base + from_right, 1).start()
            heads += [base + from_left, base + from_right]
        acc[...] += product(heads)

    def middle(k, carry):
        step(k, False)
        return carry

    lax.fori_loop(1, half - 1, middle, 0)
    step(half - 1, True)
    far = [((y + i) % ny) * nz + (z + half) % nz for i in range(ny)]
    for j in far:
        arrived(j)

    scaled = (acc[...] + product(far)) * gain_v[...]
    a_send[...] = scaled.astype(jnp.bfloat16)
    red_loc[1:2, :] = token_row(scaled * xf)
    red_y[y] = red_loc[...]

    def over_y(i):
        return remote(red_loc, red_y.at[y], ry_ss.at[i], ry_rs.at[y], dev(s, peer(i)))

    def over_y_from(i):
        src = (y + i) % ny
        return remote(red_loc, red_y.at[src], ry_ss.at[i], ry_rs.at[src], dev(s, peer(i)))

    for i in range(1, ny):
        over_y(i).start()
    a_c = remote(a_send, a_recv, hsem.at[4], hsem.at[5], dev(before, t))
    a_c.start()
    for i in range(1, ny):
        over_y_from(i).wait_recv()
    total = red_y[0]
    for i in range(1, ny):
        total = total + red_y[i]
    red_col[...] = total

    def over_z(i):
        return remote(red_col, red_z.at[z], rz_ss.at[i], rz_rs.at[z], dev(before, y * nz + (z + i) % nz))

    def over_z_from(i):
        return remote(red_col, red_z.at[i], rz_ss.at[i], rz_rs.at[i], dev(before, t))

    for i in range(nz):
        over_z(i).start()
    x_c.wait_recv()
    a_c.wait_recv()
    for i in range(nz):
        over_z_from(i).wait_recv()
    total = red_z[0]
    for i in range(1, nz):
        total = total + red_z[i]
    inv = 1.0 / jnp.sqrt(total[0:1, :] / width + 1e-05)
    pull = total[1:2, :] * inv * inv * inv / width
    inv_c = jnp.broadcast_to(inv, (tok, tok)).T
    pull_c = jnp.broadcast_to(pull, (tok, tok)).T
    for i in range(0, feats, 128):
        a = a_recv[:, i : i + 128].astype(jnp.float32)
        xi = xr_v[:, i : i + 128].astype(jnp.float32)
        out_ref[0, :, i : i + 128] = (a * inv_c - xi * pull_c).astype(jnp.bfloat16)

    spare_c.wait_send()
    x_c.wait_send()
    a_c.wait_send()
    for i in range(1, ny):
        share(i).wait_send()
        over_y(i).wait_send()
    for i in range(nz):
        over_z(i).wait_send()
    for i in range(ny):
        base = ((y + i) % ny) * nz
        for k in range(half):
            if k < half - 1 or i % 2 == 0:
                along(base + (z + nz - k) % nz, 0).wait_send()
            if k < half - 1 or i % 2 == 1:
                along(base + (z + k) % nz, 1).wait_send()


def per_device(grad_attn, w_value, probs_own, probs_spare, evicted, layer_input, gain):
    sections, tp = lax.axis_size("section"), lax.axis_size("tp")
    ny = RUN
    nz = tp // ny
    tok = probs_own.shape[2]
    hd = grad_attn.shape[3]
    feats = w_value.shape[1]
    bf16, f32 = jnp.bfloat16, jnp.float32
    dma = pltpu.SemaphoreType.DMA
    return pl.pallas_call(
        functools.partial(kernel, (sections, ny, nz, feats * tp)),
        out_shape=jax.ShapeDtypeStruct(layer_input.shape, bf16),
        in_specs=[pl.BlockSpec(memory_space=pl.ANY)] * 7,
        out_specs=pl.BlockSpec(memory_space=pltpu.VMEM),
        scratch_shapes=[
            pltpu.VMEM((tok, hd), bf16),
            pltpu.VMEM(w_value.shape[1:], bf16),
            pltpu.VMEM((tok, tok), bf16),
            pltpu.VMEM((tok, tok), bf16),
            pltpu.SMEM(evicted.shape, jnp.int32),
            pltpu.VMEM((tok, feats), bf16),
            pltpu.VMEM((1, feats), f32),
            pltpu.VMEM((tok, feats), bf16),
            pltpu.VMEM((tp, tok, hd), bf16),
            pltpu.VMEM((tok, feats), f32),
            pltpu.VMEM((tok, feats), bf16),
            pltpu.VMEM((tok, feats), bf16),
            pltpu.VMEM((8, tok), f32),
            pltpu.VMEM((ny, 8, tok), f32),
            pltpu.VMEM((8, tok), f32),
            pltpu.VMEM((nz, 8, tok), f32),
            dma((6,)),
            dma((6,)),
            dma((ny,)),
            dma((2, tp)),
            dma((tp,)),
            dma((ny,)),
            dma((ny,)),
            dma((nz,)),
            dma((nz,)),
        ],
        compiler_params=pltpu.CompilerParams(collective_id=0, has_side_effects=True),
    )(grad_attn, w_value, probs_own, probs_spare, evicted, layer_input, gain)


def solution(mesh):
    in_specs = (
        P("section", "tp", None, None),
        P("section", "tp", None),
        P("section", "tp", None, None),
        P("section", "tp", None, None),
        P("section", None),
        P("section", None, "tp"),
        P("section", "tp"),
    )
    return jax.shard_map(
        per_device, mesh=mesh, in_specs=in_specs, out_specs=P("section", None, "tp"), check_vma=False
    )
```

```python
import functools
import itertools

import jax
import jax.numpy as jnp
from jax import lax
from jax.experimental import pallas as pl
from jax.experimental.pallas import tpu as pltpu
from jax.sharding import PartitionSpec as P

RUN = 4
TREE = {0: (1,), 1: (2,), 2: (3,), 3: (4,), 4: (5, 6)}
MESH = pl.DeviceIdType.MESH


def kernel(
    sizes,
    ga_h,
    w_h,
    own_h,
    spare_h,
    ev_h,
    x_h,
    gain_h,
    out_ref,
    ga_v,
    w_v,
    own_v,
    spare_v,
    ev_s,
    x_v,
    gain_v,
    xr_v,
    gath,
    acc,
    a_send,
    a_recv,
    red_loc,
    red_all,
    lsem,
    hsem,
    y_ss,
    ring_ss,
    rsem,
    ry_ss,
    ry_rs,
):
    sections, ny, nz, width = sizes
    tok = own_h.shape[2]
    tiles = ev_h.shape[1]
    rows = tok // tiles
    feats = w_h.shape[1]
    hd = ga_h.shape[3]
    s = lax.axis_index("section")
    t = lax.axis_index("tp")
    y, z = t // nz, t % nz
    before = (s + sections - 1) % sections
    after = (s + 1) % sections
    across = (s + sections // 2) % sections

    def dev(section, tp):
        return {"section": section, "tp": tp}

    barrier = pltpu.get_barrier_semaphore()
    jumps = sorted({b - a for a, far in TREE.items() for b in far})
    sources = [dev(across, t), dev(after, t)]
    sources += [dev(s, ((y + i) % ny) * nz + z) for i in range(1, ny)]
    sources += [dev(s, y * nz + (z + d) % nz) for j in jumps for d in (j, nz - j)]
    for d in sources:
        pl.semaphore_signal(barrier, inc=1, device_id=d, device_id_type=MESH)

    local = [
        pltpu.make_async_copy(own_h.at[0, 0], own_v, lsem.at[0]),
        pltpu.make_async_copy(ga_h.at[0, 0], ga_v, lsem.at[1]),
        pltpu.make_async_copy(ev_h, ev_s, lsem.at[2]),
        pltpu.make_async_copy(x_h.at[0], x_v, lsem.at[3]),
        pltpu.make_async_copy(gain_h, gain_v, lsem.at[4]),
        pltpu.make_async_copy(w_h.at[0], w_v, lsem.at[5]),
    ]
    for c in local:
        c.start()
    pl.semaphore_wait(barrier, len(sources))

    def remote(src, dst, send, recv, d):
        return pltpu.make_async_remote_copy(
            src_ref=src, dst_ref=dst, send_sem=send, recv_sem=recv, device_id=d, device_id_type=MESH
        )

    spare_c = remote(spare_h.at[0, 0], spare_v, hsem.at[0], hsem.at[1], dev(across, t))
    spare_c.start()
    x_c = remote(x_h.at[0], xr_v, hsem.at[2], hsem.at[3], dev(before, t))

    for c in local[:5]:
        c.wait()

    def token_row(v):
        half = v[:, :128]
        for i in range(128, feats, 128):
            half = half + v[:, i : i + 128]
        return jnp.sum(half.T, axis=0, keepdims=True)

    xf = x_v[...].astype(jnp.float32)
    red_loc[...] = jnp.zeros(red_loc.shape, jnp.float32)
    red_loc[0:1, :] = token_row(xf * xf)

    spare_c.wait_recv()
    parts = []
    for i in range(tiles):
        flag = jnp.full((rows, tok), ev_s[0, i], jnp.int32)
        parts.append(
            jnp.where(
                flag == 1,
                spare_v[i * rows : (i + 1) * rows, :].astype(jnp.float32),
                own_v[i * rows : (i + 1) * rows, :].astype(jnp.float32),
            )
        )
    mixed = jnp.concatenate(parts, axis=0)
    turned = mixed.T.astype(jnp.bfloat16)
    gath[t] = jnp.dot(turned, ga_v[...], preferred_element_type=jnp.float32).astype(jnp.bfloat16)

    half = nz // 2

    def peer(i):
        return ((y + i) % ny) * nz + z

    def share(i):
        return remote(gath.at[t], gath.at[t], y_ss.at[i], rsem.at[t], dev(s, peer(i)))

    def block(i, k, way):
        return ((y + i) % ny) * nz + ((z + nz - k) % nz if way == 0 else (z + k) % nz)

    def comes(i, k, way):
        return k < half or i % 2 == way

    def onward(i, k, way):
        j = block(i, k, way)
        copies = []
        for n, far in enumerate(TREE.get(k, ())):
            if comes(i, far, way):
                step = far - k
                to = y * nz + ((z + step) % nz if way == 0 else (z + nz - step) % nz)
                copies.append(remote(gath.at[j], gath.at[j], ring_ss.at[way, n, j], rsem.at[j], dev(s, to)))
        return copies

    def arrived(j):
        remote(gath.at[j], gath.at[j], y_ss.at[0], rsem.at[j], dev(s, peer(1))).wait_recv()

    def product(heads):
        lhs = jnp.concatenate([gath[j] for j in heads], axis=1)
        rhs = jnp.concatenate([w_v[:, pl.ds(pl.multiple_of(j * hd, hd), hd)] for j in heads], axis=1)
        return lax.dot_general(lhs, rhs, (((1,), (1,)), ((), ())), preferred_element_type=jnp.float32)

    def send_on(i, k):
        for right_copy, left_copy in itertools.zip_longest(onward(i, k, 0), onward(i, k, 1)):
            for c in (right_copy, left_copy):
                if c is not None:
                    c.start()

    for i in range(1, ny):
        share(i).start()
    send_on(0, 0)
    x_c.start()
    local[5].wait()
    for i in range(1, ny):
        arrived(peer(i))
        send_on(i, 0)
    acc[...] = product([peer(i) for i in range(ny)])

    depth = {0: 0}
    for k in sorted(TREE):
        for far in TREE[k]:
            depth[far] = depth[k] + 1
    for k in sorted(range(1, half + 1), key=lambda k: (depth[k], k not in TREE, k)):
        heads = []
        for i in range(ny):
            for way in range(2):
                if comes(i, k, way):
                    arrived(block(i, k, way))
                    for c in onward(i, k, way):
                        c.start()
                    heads.append(block(i, k, way))
        acc[...] += product(heads)

    scaled = acc[...] * gain_v[...]
    a_send[...] = scaled.astype(jnp.bfloat16)
    red_loc[1:2, :] = token_row(scaled * xf)

    def share_sum(i, k):
        to = ((y + i) % ny) * nz + (z + k) % nz
        return remote(red_loc, red_all.at[t], ry_ss.at[i, k], ry_rs.at[t], dev(before, to))

    def share_sum_from(j):
        return remote(red_loc, red_all.at[j], ry_ss.at[0, 0], ry_rs.at[j], dev(before, t))

    for k in sorted(range(nz), key=lambda k: -min(k, nz - k)):
        for i in range(ny):
            share_sum(i, k).start()
    a_c = remote(a_send, a_recv, hsem.at[4], hsem.at[5], dev(before, t))
    a_c.start()
    x_c.wait_recv()
    a_c.wait_recv()
    for j in range(ny * nz):
        share_sum_from(j).wait_recv()
    total = jnp.sum(red_all[...], axis=0)
    inv = 1.0 / jnp.sqrt(total[0:1, :] / width + 1e-05)
    pull = total[1:2, :] * inv * inv * inv / width
    inv_c = jnp.broadcast_to(inv, (tok, tok)).T
    pull_c = jnp.broadcast_to(pull, (tok, tok)).T
    for i in range(0, feats, 128):
        a = a_recv[:, i : i + 128].astype(jnp.float32)
        xi = xr_v[:, i : i + 128].astype(jnp.float32)
        out_ref[0, :, i : i + 128] = (a * inv_c - xi * pull_c).astype(jnp.bfloat16)

    spare_c.wait_send()
    x_c.wait_send()
    a_c.wait_send()
    for i in range(1, ny):
        share(i).wait_send()
    for i in range(ny):
        for k in range(nz):
            share_sum(i, k).wait_send()
    for i in range(ny):
        for k in TREE:
            for way in range(2):
                for c in onward(i, k, way):
                    c.wait_send()


def per_device(grad_attn, w_value, probs_own, probs_spare, evicted, layer_input, gain):
    sections, tp = lax.axis_size("section"), lax.axis_size("tp")
    ny = RUN
    nz = tp // ny
    tok = probs_own.shape[2]
    hd = grad_attn.shape[3]
    feats = w_value.shape[1]
    bf16, f32 = jnp.bfloat16, jnp.float32
    dma = pltpu.SemaphoreType.DMA
    return pl.pallas_call(
        functools.partial(kernel, (sections, ny, nz, feats * tp)),
        out_shape=jax.ShapeDtypeStruct(layer_input.shape, bf16),
        in_specs=[pl.BlockSpec(memory_space=pl.ANY)] * 7,
        out_specs=pl.BlockSpec(memory_space=pltpu.VMEM),
        scratch_shapes=[
            pltpu.VMEM((tok, hd), bf16),
            pltpu.VMEM(w_value.shape[1:], bf16),
            pltpu.VMEM((tok, tok), bf16),
            pltpu.VMEM((tok, tok), bf16),
            pltpu.SMEM(evicted.shape, jnp.int32),
            pltpu.VMEM((tok, feats), bf16),
            pltpu.VMEM((1, feats), f32),
            pltpu.VMEM((tok, feats), bf16),
            pltpu.VMEM((tp, tok, hd), bf16),
            pltpu.VMEM((tok, feats), f32),
            pltpu.VMEM((tok, feats), bf16),
            pltpu.VMEM((tok, feats), bf16),
            pltpu.VMEM((2, tok), f32),
            pltpu.VMEM((tp, 2, tok), f32),
            dma((6,)),
            dma((6,)),
            dma((ny,)),
            dma((2, max(len(far) for far in TREE.values()), tp)),
            dma((tp,)),
            dma((ny, nz)),
            dma((tp,)),
        ],
        compiler_params=pltpu.CompilerParams(collective_id=0, has_side_effects=True),
    )(grad_attn, w_value, probs_own, probs_spare, evicted, layer_input, gain)


def solution(mesh):
    in_specs = (
        P("section", "tp", None, None),
        P("section", "tp", None),
        P("section", "tp", None, None),
        P("section", "tp", None, None),
        P("section", None),
        P("section", None, "tp"),
        P("section", "tp"),
    )
    return jax.shard_map(
        per_device, mesh=mesh, in_specs=in_specs, out_specs=P("section", None, "tp"), check_vma=False
    )
```

```python
import functools
import itertools

import jax
import jax.numpy as jnp
from jax import lax
from jax.experimental import pallas as pl
from jax.experimental.pallas import tpu as pltpu
from jax.sharding import PartitionSpec as P

RUN = 4
TREE = {0: (2, 1), 2: (4, 3), 4: (5, 6)}
BOTH = (1,)
WIDEST = max(len(far) for far in TREE.values())
MESH = pl.DeviceIdType.MESH


def kernel(
    sizes,
    ga_h,
    w_h,
    own_h,
    spare_h,
    ev_h,
    x_h,
    gain_h,
    out_ref,
    ga_v,
    w_v,
    own_v,
    spare_v,
    ev_s,
    x_v,
    gain_v,
    xr_v,
    gath,
    acc,
    a_send,
    a_recv,
    red_loc,
    red_all,
    lsem,
    hsem,
    y_ss,
    ring_ss,
    rsem,
    ry_ss,
    ry_rs,
):
    sections, ny, nz, width = sizes
    tok = own_h.shape[2]
    tiles = ev_h.shape[1]
    rows = tok // tiles
    feats = w_h.shape[1]
    hd = ga_h.shape[3]
    s = lax.axis_index("section")
    t = lax.axis_index("tp")
    y, z = t // nz, t % nz
    before = (s + sections - 1) % sections
    after = (s + 1) % sections
    across = (s + sections // 2) % sections

    def dev(section, tp):
        return {"section": section, "tp": tp}

    barrier = pltpu.get_barrier_semaphore()
    jumps = sorted({b - a for a, far in TREE.items() for b in far})
    sources = [dev(across, t), dev(after, t)]
    beside = y + 1 - 2 * (y % 2)
    rows_of = [y, beside, (y + 2) % ny, (beside + 2) % ny]
    sources += [dev(s, rows_of[i] * nz + z) for i in range(1, ny)]
    sources += [dev(s, y * nz + (z + d) % nz) for j in jumps for d in (j, nz - j)]
    for d in sources:
        pl.semaphore_signal(barrier, inc=1, device_id=d, device_id_type=MESH)

    local = [
        pltpu.make_async_copy(own_h.at[0, 0], own_v, lsem.at[0]),
        pltpu.make_async_copy(ga_h.at[0, 0], ga_v, lsem.at[1]),
        pltpu.make_async_copy(ev_h, ev_s, lsem.at[2]),
        pltpu.make_async_copy(x_h.at[0], x_v, lsem.at[3]),
        pltpu.make_async_copy(gain_h, gain_v, lsem.at[4]),
        pltpu.make_async_copy(w_h.at[0], w_v, lsem.at[5]),
    ]
    for c in local:
        c.start()
    pl.semaphore_wait(barrier, len(sources))

    def remote(src, dst, send, recv, d):
        return pltpu.make_async_remote_copy(
            src_ref=src, dst_ref=dst, send_sem=send, recv_sem=recv, device_id=d, device_id_type=MESH
        )

    spare_c = remote(spare_h.at[0, 0], spare_v, hsem.at[0], hsem.at[1], dev(across, t))
    spare_c.start()
    x_c = remote(x_h.at[0], xr_v, hsem.at[2], hsem.at[3], dev(before, t))

    x_c.start()

    for c in local[:5]:
        c.wait()

    def token_row(v):
        half = v[:, :128]
        for i in range(128, feats, 128):
            half = half + v[:, i : i + 128]
        return jnp.sum(half.T, axis=0, keepdims=True)

    xf = x_v[...].astype(jnp.float32)
    red_loc[...] = jnp.zeros(red_loc.shape, jnp.float32)
    red_loc[0:1, :] = token_row(xf * xf)

    spare_c.wait_recv()
    parts = []
    for i in range(tiles):
        flag = jnp.full((rows, tok), ev_s[0, i], jnp.int32)
        parts.append(
            jnp.where(
                flag == 1,
                spare_v[i * rows : (i + 1) * rows, :].astype(jnp.float32),
                own_v[i * rows : (i + 1) * rows, :].astype(jnp.float32),
            )
        )
    mixed = jnp.concatenate(parts, axis=0)
    turned = mixed.T.astype(jnp.bfloat16)
    gath[t] = jnp.dot(turned, ga_v[...], preferred_element_type=jnp.float32).astype(jnp.bfloat16)

    half = nz // 2

    def peer(i):
        return rows_of[i] * nz + z

    def share(i):
        return remote(gath.at[t], gath.at[t], y_ss.at[i], rsem.at[t], dev(s, peer(i)))

    def block(i, k, way):
        return rows_of[i] * nz + ((z + nz - k) % nz if way == 0 else (z + k) % nz)

    def comes(i, k, way):
        return k < half or i // 2 == way

    def travels(i, k):
        return i % 2 == 0 or k in BOTH

    def onward(i, k, way):
        j = block(i, k, way)
        copies = []
        for n, far in enumerate(TREE.get(k, ())):
            if comes(i, far, way) and travels(i, far):
                step = far - k
                to = y * nz + ((z + step) % nz if way == 0 else (z + nz - step) % nz)
                copies.append(remote(gath.at[j], gath.at[j], ring_ss.at[way, n, j], rsem.at[j], dev(s, to)))
        if k and i % 2 == 0 and not travels(i + 1, k):
            to = beside * nz + z
            copies.append(remote(gath.at[j], gath.at[j], ring_ss.at[way, WIDEST, j], rsem.at[j], dev(s, to)))
        return copies

    def arrived(j):
        remote(gath.at[j], gath.at[j], y_ss.at[0], rsem.at[j], dev(s, peer(1))).wait_recv()

    def product(heads):
        lhs = jnp.concatenate([gath[j] for j in heads], axis=1)
        rhs = jnp.concatenate([w_v[:, pl.ds(pl.multiple_of(j * hd, hd), hd)] for j in heads], axis=1)
        return lax.dot_general(lhs, rhs, (((1,), (1,)), ((), ())), preferred_element_type=jnp.float32)

    def send_on(i, k):
        for right_copy, left_copy in itertools.zip_longest(onward(i, k, 0), onward(i, k, 1)):
            for c in (right_copy, left_copy):
                if c is not None:
                    c.start()

    for i in (2, 1, 3):
        share(i).start()
    send_on(0, 0)
    local[5].wait()
    for i in (2, 1, 3):
        arrived(peer(i))
        send_on(i, 0)
    acc[...] = product([peer(i) for i in range(ny)])

    depth = {0: 0}
    for k in sorted(TREE):
        for far in TREE[k]:
            depth[far] = depth[k] + 1
    order = sorted(range(1, half + 1), key=lambda k: (depth[k], k not in TREE, k))
    handed = []
    for k in order:
        heads = []
        for i in (0, 2, 1, 3):
            for way in range(2):
                if comes(i, k, way):
                    if travels(i, k):
                        arrived(block(i, k, way))
                        for c in onward(i, k, way):
                            c.start()
                        heads.append(block(i, k, way))
                    else:
                        handed.append(block(i, k, way))
        acc[...] += product(heads)
    for j in handed:
        arrived(j)
    acc[...] += product(handed)

    scaled = acc[...] * gain_v[...]
    a_send[...] = scaled.astype(jnp.bfloat16)
    red_loc[1:2, :] = token_row(scaled * xf)

    def share_sum(i, k):
        to = rows_of[i] * nz + (z + k) % nz
        return remote(red_loc, red_all.at[t], ry_ss.at[i, k], ry_rs.at[t], dev(before, to))

    def share_sum_from(j):
        return remote(red_loc, red_all.at[j], ry_ss.at[0, 0], ry_rs.at[j], dev(before, t))

    for k in sorted(range(nz), key=lambda k: -min(k, nz - k)):
        for i in range(ny):
            share_sum(i, k).start()
    a_c = remote(a_send, a_recv, hsem.at[4], hsem.at[5], dev(before, t))
    a_c.start()
    x_c.wait_recv()
    a_c.wait_recv()
    for j in range(ny * nz):
        share_sum_from(j).wait_recv()
    total = jnp.sum(red_all[...], axis=0)
    inv = 1.0 / jnp.sqrt(total[0:1, :] / width + 1e-05)
    pull = total[1:2, :] * inv * inv * inv / width
    inv_c = jnp.broadcast_to(inv, (tok, tok)).T
    pull_c = jnp.broadcast_to(pull, (tok, tok)).T
    for i in range(0, feats, 128):
        a = a_recv[:, i : i + 128].astype(jnp.float32)
        xi = xr_v[:, i : i + 128].astype(jnp.float32)
        out_ref[0, :, i : i + 128] = (a * inv_c - xi * pull_c).astype(jnp.bfloat16)

    spare_c.wait_send()
    x_c.wait_send()
    a_c.wait_send()
    for i in range(1, ny):
        share(i).wait_send()
    for i in range(ny):
        for k in range(nz):
            share_sum(i, k).wait_send()
    for i in range(ny):
        for k in range(half + 1):
            for way in range(2):
                if comes(i, k, way) and (k == 0 or travels(i, k)):
                    for c in onward(i, k, way):
                        c.wait_send()


def per_device(grad_attn, w_value, probs_own, probs_spare, evicted, layer_input, gain):
    sections, tp = lax.axis_size("section"), lax.axis_size("tp")
    ny = RUN
    nz = tp // ny
    tok = probs_own.shape[2]
    hd = grad_attn.shape[3]
    feats = w_value.shape[1]
    bf16, f32 = jnp.bfloat16, jnp.float32
    dma = pltpu.SemaphoreType.DMA
    return pl.pallas_call(
        functools.partial(kernel, (sections, ny, nz, feats * tp)),
        out_shape=jax.ShapeDtypeStruct(layer_input.shape, bf16),
        in_specs=[pl.BlockSpec(memory_space=pl.ANY)] * 7,
        out_specs=pl.BlockSpec(memory_space=pltpu.VMEM),
        scratch_shapes=[
            pltpu.VMEM((tok, hd), bf16),
            pltpu.VMEM(w_value.shape[1:], bf16),
            pltpu.VMEM((tok, tok), bf16),
            pltpu.VMEM((tok, tok), bf16),
            pltpu.SMEM(evicted.shape, jnp.int32),
            pltpu.VMEM((tok, feats), bf16),
            pltpu.VMEM((1, feats), f32),
            pltpu.VMEM((tok, feats), bf16),
            pltpu.VMEM((tp, tok, hd), bf16),
            pltpu.VMEM((tok, feats), f32),
            pltpu.VMEM((tok, feats), bf16),
            pltpu.VMEM((tok, feats), bf16),
            pltpu.VMEM((2, tok), f32),
            pltpu.VMEM((tp, 2, tok), f32),
            dma((6,)),
            dma((6,)),
            dma((ny,)),
            dma((2, WIDEST + 1, tp)),
            dma((tp,)),
            dma((ny, nz)),
            dma((tp,)),
        ],
        compiler_params=pltpu.CompilerParams(collective_id=0, has_side_effects=True),
    )(grad_attn, w_value, probs_own, probs_spare, evicted, layer_input, gain)


def solution(mesh):
    in_specs = (
        P("section", "tp", None, None),
        P("section", "tp", None),
        P("section", "tp", None, None),
        P("section", "tp", None, None),
        P("section", None),
        P("section", None, "tp"),
        P("section", "tp"),
    )
    return jax.shard_map(
        per_device, mesh=mesh, in_specs=in_specs, out_specs=P("section", None, "tp"), check_vma=False
    )
```

```python
import functools
import itertools

import jax
import jax.numpy as jnp
from jax import lax
from jax.experimental import pallas as pl
from jax.experimental.pallas import tpu as pltpu
from jax.sharding import PartitionSpec as P

RUN = 4
TREE = {0: (2, 1), 2: (4, 3), 4: (5, 6)}
BOTH = (1,)
BEHIND = 2
WIDEST = max(len(far) for far in TREE.values())
MESH = pl.DeviceIdType.MESH


def kernel(
    sizes,
    ga_h,
    w_h,
    own_h,
    spare_h,
    ev_h,
    x_h,
    gain_h,
    out_ref,
    ga_v,
    w_v,
    own_v,
    spare_v,
    ev_s,
    x_v,
    gain_v,
    xr_v,
    gath,
    acc,
    a_send,
    a_recv,
    red_loc,
    red_all,
    lsem,
    hsem,
    y_ss,
    ring_ss,
    rsem,
    ry_ss,
    ry_rs,
):
    sections, ny, nz, width = sizes
    tok = own_h.shape[2]
    tiles = ev_h.shape[1]
    rows = tok // tiles
    feats = w_h.shape[1]
    hd = ga_h.shape[3]
    s = lax.axis_index("section")
    t = lax.axis_index("tp")
    y, z = t // nz, t % nz
    before = (s + sections - 1) % sections
    after = (s + 1) % sections
    across = (s + sections // 2) % sections

    def dev(section, tp):
        return {"section": section, "tp": tp}

    barrier = pltpu.get_barrier_semaphore()
    jumps = sorted({b - a for a, far in TREE.items() for b in far})
    sources = [dev(across, t), dev(after, t)]
    beside = y + 1 - 2 * (y % 2)
    rows_of = [y, beside, (y + 2) % ny, (beside + 2) % ny]
    sources += [dev(s, rows_of[i] * nz + z) for i in range(1, ny)]
    sources += [dev(s, y * nz + (z + d) % nz) for j in jumps for d in (j, nz - j)]
    for d in sources:
        pl.semaphore_signal(barrier, inc=1, device_id=d, device_id_type=MESH)

    local = [
        pltpu.make_async_copy(own_h.at[0, 0], own_v, lsem.at[0]),
        pltpu.make_async_copy(ga_h.at[0, 0], ga_v, lsem.at[1]),
        pltpu.make_async_copy(ev_h, ev_s, lsem.at[2]),
        pltpu.make_async_copy(x_h.at[0], x_v, lsem.at[3]),
        pltpu.make_async_copy(gain_h, gain_v, lsem.at[4]),
        pltpu.make_async_copy(w_h.at[0], w_v, lsem.at[5]),
    ]
    for c in local:
        c.start()
    pl.semaphore_wait(barrier, len(sources))

    def remote(src, dst, send, recv, d):
        return pltpu.make_async_remote_copy(
            src_ref=src, dst_ref=dst, send_sem=send, recv_sem=recv, device_id=d, device_id_type=MESH
        )

    spare_c = remote(spare_h.at[0, 0], spare_v, hsem.at[0], hsem.at[1], dev(across, t))
    spare_c.start()
    x_c = remote(x_h.at[0], xr_v, hsem.at[2], hsem.at[3], dev(before, t))

    x_c.start()

    for c in local[:5]:
        c.wait()

    def token_row(v):
        half = v[:, :128]
        for i in range(128, feats, 128):
            half = half + v[:, i : i + 128]
        return jnp.sum(half.T, axis=0, keepdims=True)

    xf = x_v[...].astype(jnp.float32)
    red_loc[...] = jnp.zeros(red_loc.shape, jnp.float32)
    red_loc[0:1, :] = token_row(xf * xf)

    spare_c.wait_recv()
    parts = []
    for i in range(tiles):
        flag = jnp.full((rows, tok), ev_s[0, i], jnp.int32)
        parts.append(
            jnp.where(
                flag == 1,
                spare_v[i * rows : (i + 1) * rows, :].astype(jnp.float32),
                own_v[i * rows : (i + 1) * rows, :].astype(jnp.float32),
            )
        )
    mixed = jnp.concatenate(parts, axis=0)
    turned = mixed.T.astype(jnp.bfloat16)
    gath[t] = jnp.dot(turned, ga_v[...], preferred_element_type=jnp.float32).astype(jnp.bfloat16)

    half = nz // 2

    def peer(i):
        return rows_of[i] * nz + z

    def share(i):
        return remote(gath.at[t], gath.at[t], y_ss.at[i], rsem.at[t], dev(s, peer(i)))

    def block(i, k, way):
        return rows_of[i] * nz + ((z + nz - k) % nz if way == 0 else (z + k) % nz)

    def comes(i, k, way):
        return k < half or i // 2 == way

    def travels(i, k):
        return i % 2 == 0 or k in BOTH

    def onward(i, k, way):
        j = block(i, k, way)
        copies = []
        for n, far in enumerate(TREE.get(k, ())):
            if comes(i, far, way) and travels(i, far):
                step = far - k
                to = y * nz + ((z + step) % nz if way == 0 else (z + nz - step) % nz)
                copies.append(remote(gath.at[j], gath.at[j], ring_ss.at[way, n, j], rsem.at[j], dev(s, to)))
        if k and i % 2 == 0 and not travels(i + 1, k):
            to = beside * nz + z
            copies.append(remote(gath.at[j], gath.at[j], ring_ss.at[way, WIDEST, j], rsem.at[j], dev(s, to)))
        return copies

    def arrived(j):
        remote(gath.at[j], gath.at[j], y_ss.at[0], rsem.at[j], dev(s, peer(1))).wait_recv()

    def product(heads):
        lhs = jnp.concatenate([gath[j] for j in heads], axis=1)
        rhs = jnp.concatenate([w_v[:, pl.ds(pl.multiple_of(j * hd, hd), hd)] for j in heads], axis=1)
        return lax.dot_general(lhs, rhs, (((1,), (1,)), ((), ())), preferred_element_type=jnp.float32)

    def send_on(i, k):
        for right_copy, left_copy in itertools.zip_longest(onward(i, k, 0), onward(i, k, 1)):
            for c in (right_copy, left_copy):
                if c is not None:
                    c.start()

    for i in (2, 1, 3):
        share(i).start()
    send_on(0, 0)
    local[5].wait()
    for i in (2, 1, 3):
        arrived(peer(i))
        send_on(i, 0)
    acc[...] = product([peer(i) for i in range(ny)])

    depth = {0: 0}
    for k in sorted(TREE):
        for far in TREE[k]:
            depth[far] = depth[k] + 1
    order = sorted(range(1, half + 1), key=lambda k: (depth[k], k not in TREE, k))
    waiting = []
    for k in order:
        heads, handed = [], []
        for i in (0, 2, 1, 3):
            for way in range(2):
                if comes(i, k, way):
                    if travels(i, k):
                        arrived(block(i, k, way))
                        for c in onward(i, k, way):
                            c.start()
                        heads.append(block(i, k, way))
                    else:
                        handed.append(block(i, k, way))
        waiting.append(handed)
        if len(waiting) > BEHIND:
            for j in waiting[0]:
                arrived(j)
            heads += waiting.pop(0)
        acc[...] += product(heads)
    for handed in waiting:
        for j in handed:
            arrived(j)
        if handed:
            acc[...] += product(handed)

    scaled = acc[...] * gain_v[...]
    a_send[...] = scaled.astype(jnp.bfloat16)
    red_loc[1:2, :] = token_row(scaled * xf)

    def share_sum(i, k):
        to = rows_of[i] * nz + (z + k) % nz
        return remote(red_loc, red_all.at[t], ry_ss.at[i, k], ry_rs.at[t], dev(before, to))

    def share_sum_from(j):
        return remote(red_loc, red_all.at[j], ry_ss.at[0, 0], ry_rs.at[j], dev(before, t))

    for k in sorted(range(nz), key=lambda k: -min(k, nz - k)):
        for i in range(ny):
            share_sum(i, k).start()
    a_c = remote(a_send, a_recv, hsem.at[4], hsem.at[5], dev(before, t))
    a_c.start()
    x_c.wait_recv()
    a_c.wait_recv()
    for j in range(ny * nz):
        share_sum_from(j).wait_recv()
    total = jnp.sum(red_all[...], axis=0)
    inv = 1.0 / jnp.sqrt(total[0:1, :] / width + 1e-05)
    pull = total[1:2, :] * inv * inv * inv / width
    inv_c = jnp.broadcast_to(inv, (tok, tok)).T
    pull_c = jnp.broadcast_to(pull, (tok, tok)).T
    for i in range(0, feats, 128):
        a = a_recv[:, i : i + 128].astype(jnp.float32)
        xi = xr_v[:, i : i + 128].astype(jnp.float32)
        out_ref[0, :, i : i + 128] = (a * inv_c - xi * pull_c).astype(jnp.bfloat16)

    spare_c.wait_send()
    x_c.wait_send()
    a_c.wait_send()
    for i in range(1, ny):
        share(i).wait_send()
    for i in range(ny):
        for k in range(nz):
            share_sum(i, k).wait_send()
    for i in range(ny):
        for k in range(half + 1):
            for way in range(2):
                if comes(i, k, way) and (k == 0 or travels(i, k)):
                    for c in onward(i, k, way):
                        c.wait_send()


def per_device(grad_attn, w_value, probs_own, probs_spare, evicted, layer_input, gain):
    sections, tp = lax.axis_size("section"), lax.axis_size("tp")
    ny = RUN
    nz = tp // ny
    tok = probs_own.shape[2]
    hd = grad_attn.shape[3]
    feats = w_value.shape[1]
    bf16, f32 = jnp.bfloat16, jnp.float32
    dma = pltpu.SemaphoreType.DMA
    return pl.pallas_call(
        functools.partial(kernel, (sections, ny, nz, feats * tp)),
        out_shape=jax.ShapeDtypeStruct(layer_input.shape, bf16),
        in_specs=[pl.BlockSpec(memory_space=pl.ANY)] * 7,
        out_specs=pl.BlockSpec(memory_space=pltpu.VMEM),
        scratch_shapes=[
            pltpu.VMEM((tok, hd), bf16),
            pltpu.VMEM(w_value.shape[1:], bf16),
            pltpu.VMEM((tok, tok), bf16),
            pltpu.VMEM((tok, tok), bf16),
            pltpu.SMEM(evicted.shape, jnp.int32),
            pltpu.VMEM((tok, feats), bf16),
            pltpu.VMEM((1, feats), f32),
            pltpu.VMEM((tok, feats), bf16),
            pltpu.VMEM((tp, tok, hd), bf16),
            pltpu.VMEM((tok, feats), f32),
            pltpu.VMEM((tok, feats), bf16),
            pltpu.VMEM((tok, feats), bf16),
            pltpu.VMEM((2, tok), f32),
            pltpu.VMEM((tp, 2, tok), f32),
            dma((6,)),
            dma((6,)),
            dma((ny,)),
            dma((2, WIDEST + 1, tp)),
            dma((tp,)),
            dma((ny, nz)),
            dma((tp,)),
        ],
        compiler_params=pltpu.CompilerParams(collective_id=0, has_side_effects=True),
    )(grad_attn, w_value, probs_own, probs_spare, evicted, layer_input, gain)


def solution(mesh):
    in_specs = (
        P("section", "tp", None, None),
        P("section", "tp", None),
        P("section", "tp", None, None),
        P("section", "tp", None, None),
        P("section", None),
        P("section", None, "tp"),
        P("section", "tp"),
    )
    return jax.shard_map(
        per_device, mesh=mesh, in_specs=in_specs, out_specs=P("section", None, "tp"), check_vma=False
    )
```

```python
import functools
import itertools

import jax
import jax.numpy as jnp
from jax import lax
from jax.experimental import pallas as pl
from jax.experimental.pallas import tpu as pltpu
from jax.sharding import PartitionSpec as P

RUN = 4
TREE = {0: (2, 1), 2: (4, 3), 4: (5, 6)}
BOTH = (1,)
BEHIND = 2
WIDEST = max(len(far) for far in TREE.values())
MESH = pl.DeviceIdType.MESH


def kernel(
    sizes,
    ga_h,
    w_h,
    own_h,
    spare_h,
    ev_h,
    x_h,
    gain_h,
    out_ref,
    ga_v,
    w_v,
    own_v,
    spare_v,
    ev_s,
    x_v,
    gain_v,
    xr_v,
    gath,
    acc,
    a_send,
    a_recv,
    red_loc,
    red_all,
    lsem,
    hsem,
    y_ss,
    ring_ss,
    rsem,
    ry_ss,
    ry_rs,
):
    sections, ny, nz, width = sizes
    tok = own_h.shape[2]
    tiles = ev_h.shape[1]
    rows = tok // tiles
    feats = w_h.shape[1]
    hd = ga_h.shape[3]
    s = lax.axis_index("section")
    t = lax.axis_index("tp")
    y, z = t // nz, t % nz
    before = (s + sections - 1) % sections
    after = (s + 1) % sections
    across = (s + sections // 2) % sections

    def dev(section, tp):
        return {"section": section, "tp": tp}

    barrier = pltpu.get_barrier_semaphore()
    jumps = sorted({b - a for a, far in TREE.items() for b in far})
    sources = [dev(across, t), dev(after, t)]
    beside = y + 1 - 2 * (y % 2)
    rows_of = [y, beside, (y + 2) % ny, (beside + 2) % ny]
    sources += [dev(s, rows_of[i] * nz + z) for i in range(1, ny)]
    sources += [dev(s, y * nz + (z + d) % nz) for j in jumps for d in (j, nz - j)]
    for d in sources:
        pl.semaphore_signal(barrier, inc=1, device_id=d, device_id_type=MESH)

    local = [
        pltpu.make_async_copy(own_h.at[0, 0], own_v, lsem.at[0]),
        pltpu.make_async_copy(ga_h.at[0, 0], ga_v, lsem.at[1]),
        pltpu.make_async_copy(ev_h, ev_s, lsem.at[2]),
        pltpu.make_async_copy(x_h.at[0], x_v, lsem.at[3]),
        pltpu.make_async_copy(gain_h, gain_v, lsem.at[4]),
        pltpu.make_async_copy(w_h.at[0], w_v, lsem.at[5]),
    ]
    for c in local:
        c.start()
    pl.semaphore_wait(barrier, len(sources))

    def remote(src, dst, send, recv, d):
        return pltpu.make_async_remote_copy(
            src_ref=src, dst_ref=dst, send_sem=send, recv_sem=recv, device_id=d, device_id_type=MESH
        )

    spare_c = remote(spare_h.at[0, 0], spare_v, hsem.at[0], hsem.at[1], dev(across, t))
    spare_c.start()
    x_c = remote(x_h.at[0], xr_v, hsem.at[2], hsem.at[3], dev(before, t))

    x_c.start()

    for c in local[:5]:
        c.wait()

    def token_row(v):
        half = v[:, :128]
        for i in range(128, feats, 128):
            half = half + v[:, i : i + 128]
        return jnp.sum(half.T, axis=0, keepdims=True)

    xf = x_v[...].astype(jnp.float32)
    red_loc[...] = jnp.zeros(red_loc.shape, jnp.float32)
    red_loc[0:1, :] = token_row(xf * xf)

    spare_c.wait_recv()
    parts = []
    for i in range(tiles):
        flag = jnp.full((rows, tok), ev_s[0, i], jnp.int32)
        parts.append(
            jnp.where(
                flag == 1,
                spare_v[i * rows : (i + 1) * rows, :].astype(jnp.float32),
                own_v[i * rows : (i + 1) * rows, :].astype(jnp.float32),
            )
        )
    mixed = jnp.concatenate(parts, axis=0)
    turned = mixed.T.astype(jnp.bfloat16)
    gath[t] = jnp.dot(turned, ga_v[...], preferred_element_type=jnp.float32).astype(jnp.bfloat16)

    half = nz // 2

    def peer(i):
        return rows_of[i] * nz + z

    def share(i):
        return remote(gath.at[t], gath.at[t], y_ss.at[i], rsem.at[t], dev(s, peer(i)))

    def block(i, k, way):
        return rows_of[i] * nz + ((z + nz - k) % nz if way == 0 else (z + k) % nz)

    def comes(i, k, way):
        return k < half or i // 2 == way

    def travels(i, k):
        return i % 2 == 0 or k in BOTH

    def onward(i, k, way):
        j = block(i, k, way)
        copies = []
        for n, far in enumerate(TREE.get(k, ())):
            if comes(i, far, way) and travels(i, far):
                step = far - k
                to = y * nz + ((z + step) % nz if way == 0 else (z + nz - step) % nz)
                copies.append(remote(gath.at[j], gath.at[j], ring_ss.at[way, n, j], rsem.at[j], dev(s, to)))
        if k and i % 2 == 0 and not travels(i + 1, k):
            to = beside * nz + z
            copies.append(remote(gath.at[j], gath.at[j], ring_ss.at[way, WIDEST, j], rsem.at[j], dev(s, to)))
        return copies

    def arrived(j):
        remote(gath.at[j], gath.at[j], y_ss.at[0], rsem.at[j], dev(s, peer(1))).wait_recv()

    def product(heads):
        lhs = jnp.concatenate([gath[j] for j in heads], axis=1)
        rhs = jnp.concatenate([w_v[:, pl.ds(pl.multiple_of(j * hd, hd), hd)] for j in heads], axis=1)
        return lax.dot_general(lhs, rhs, (((1,), (1,)), ((), ())), preferred_element_type=jnp.float32)

    def send_on(i, k):
        for right_copy, left_copy in itertools.zip_longest(onward(i, k, 0), onward(i, k, 1)):
            for c in (right_copy, left_copy):
                if c is not None:
                    c.start()

    for i in (2, 1, 3):
        share(i).start()
    send_on(0, 0)
    local[5].wait()
    for i in (2, 1, 3):
        arrived(peer(i))
        send_on(i, 0)
    acc[...] = product([peer(i) for i in range(ny)])

    depth = {0: 0}
    for k in sorted(TREE):
        for far in TREE[k]:
            depth[far] = depth[k] + 1
    order = sorted(range(1, half + 1), key=lambda k: (depth[k], k not in TREE, k))
    waiting = []
    for k in order:
        heads, handed = [], []
        for i in (0, 2, 1, 3):
            for way in range(2):
                if comes(i, k, way):
                    if travels(i, k):
                        arrived(block(i, k, way))
                        for c in onward(i, k, way):
                            c.start()
                        heads.append(block(i, k, way))
                    else:
                        handed.append(block(i, k, way))
        waiting.append(handed)
        if len(waiting) > BEHIND:
            for j in waiting[0]:
                arrived(j)
            heads += waiting.pop(0)
        acc[...] += product(heads)
    for handed in waiting:
        for j in handed:
            arrived(j)
        if handed:
            acc[...] += product(handed)

    scaled = acc[...] * gain_v[...]
    a_send[...] = scaled.astype(jnp.bfloat16)
    a_c = remote(a_send, a_recv, hsem.at[4], hsem.at[5], dev(before, t))
    a_c.start()
    red_loc[1:2, :] = token_row(scaled * xf)

    def share_sum(i, k):
        to = rows_of[i] * nz + (z + k) % nz
        return remote(red_loc, red_all.at[t], ry_ss.at[i, k], ry_rs.at[t], dev(before, to))

    def share_sum_from(j):
        return remote(red_loc, red_all.at[j], ry_ss.at[0, 0], ry_rs.at[j], dev(before, t))

    for k in sorted(range(nz), key=lambda k: -min(k, nz - k)):
        for i in range(ny):
            share_sum(i, k).start()
    x_c.wait_recv()
    a_c.wait_recv()
    for j in range(ny * nz):
        share_sum_from(j).wait_recv()
    total = jnp.sum(red_all[...], axis=0)
    inv = 1.0 / jnp.sqrt(total[0:1, :] / width + 1e-05)
    pull = total[1:2, :] * inv * inv * inv / width
    inv_c = jnp.broadcast_to(inv, (tok, tok)).T
    pull_c = jnp.broadcast_to(pull, (tok, tok)).T
    for i in range(0, feats, 128):
        a = a_recv[:, i : i + 128].astype(jnp.float32)
        xi = xr_v[:, i : i + 128].astype(jnp.float32)
        out_ref[0, :, i : i + 128] = (a * inv_c - xi * pull_c).astype(jnp.bfloat16)

    spare_c.wait_send()
    x_c.wait_send()
    a_c.wait_send()
    for i in range(1, ny):
        share(i).wait_send()
    for i in range(ny):
        for k in range(nz):
            share_sum(i, k).wait_send()
    for i in range(ny):
        for k in range(half + 1):
            for way in range(2):
                if comes(i, k, way) and (k == 0 or travels(i, k)):
                    for c in onward(i, k, way):
                        c.wait_send()


def per_device(grad_attn, w_value, probs_own, probs_spare, evicted, layer_input, gain):
    sections, tp = lax.axis_size("section"), lax.axis_size("tp")
    ny = RUN
    nz = tp // ny
    tok = probs_own.shape[2]
    hd = grad_attn.shape[3]
    feats = w_value.shape[1]
    bf16, f32 = jnp.bfloat16, jnp.float32
    dma = pltpu.SemaphoreType.DMA
    return pl.pallas_call(
        functools.partial(kernel, (sections, ny, nz, feats * tp)),
        out_shape=jax.ShapeDtypeStruct(layer_input.shape, bf16),
        in_specs=[pl.BlockSpec(memory_space=pl.ANY)] * 7,
        out_specs=pl.BlockSpec(memory_space=pltpu.VMEM),
        scratch_shapes=[
            pltpu.VMEM((tok, hd), bf16),
            pltpu.VMEM(w_value.shape[1:], bf16),
            pltpu.VMEM((tok, tok), bf16),
            pltpu.VMEM((tok, tok), bf16),
            pltpu.SMEM(evicted.shape, jnp.int32),
            pltpu.VMEM((tok, feats), bf16),
            pltpu.VMEM((1, feats), f32),
            pltpu.VMEM((tok, feats), bf16),
            pltpu.VMEM((tp, tok, hd), bf16),
            pltpu.VMEM((tok, feats), f32),
            pltpu.VMEM((tok, feats), bf16),
            pltpu.VMEM((tok, feats), bf16),
            pltpu.VMEM((2, tok), f32),
            pltpu.VMEM((tp, 2, tok), f32),
            dma((6,)),
            dma((6,)),
            dma((ny,)),
            dma((2, WIDEST + 1, tp)),
            dma((tp,)),
            dma((ny, nz)),
            dma((tp,)),
        ],
        compiler_params=pltpu.CompilerParams(collective_id=0, has_side_effects=True),
    )(grad_attn, w_value, probs_own, probs_spare, evicted, layer_input, gain)


def solution(mesh):
    in_specs = (
        P("section", "tp", None, None),
        P("section", "tp", None),
        P("section", "tp", None, None),
        P("section", "tp", None, None),
        P("section", None),
        P("section", None, "tp"),
        P("section", "tp"),
    )
    return jax.shard_map(
        per_device, mesh=mesh, in_specs=in_specs, out_specs=P("section", None, "tp"), check_vma=False
    )
```
